32 devices in a mesh: rep: 16 (over z, x, core), shard: 2 (over y).
Axes of the slice: x: 2, y: 2, z: 4, core: 2. Of those that a mesh axis runs over, the one named last changes fastest.
Arguments:
- layer_input: bfloat16 [24576, 1024], P(('rep', 'shard')), may hold values from -6 to 6
- output_gradient: bfloat16 [24576, 1024], P(('rep', 'shard')), may hold values from -6 to 6
- routes: int32 [24576, 8], P(('rep', 'shard')), may hold values from 0 to 31, all different within a row; in each aligned block of 768 rows (0 to 767, 768 to 1535, ...) at most 240 rows name the same one
- sequence_adapter: int32 [16, 2], P('rep'), may hold values from 0 to 3
- attention_gain: float32 [1024], replicated, may hold values from 0.1 to 1.9
- experts_gain: float32 [1024], replicated, may hold values from 0.1 to 1.9
- project_weight: bfloat16 [1024, 2048], P(None, 'shard'), may hold values from -0.25 to 0.25
- output_weight: bfloat16 [1024, 1024], P('shard'), may hold values from -0.75 to 0.75
- router_weight: bfloat16 [1024, 32], P('shard'), may hold values from -0.09375 to 0.09375
- adapter_project_first: bfloat16 [1024, 192], P('shard'), may hold values from -0.1875 to 0.1875
- adapter_project_second: bfloat16 [64, 2048], P(None, 'shard'), may hold values from -0.75 to 0.75
- adapter_output_first: bfloat16 [1024, 64], P('shard'), may hold values from -0.75 to 0.75
- adapter_output_second: bfloat16 [64, 1024], P(None, 'shard'), may hold values from -0.75 to 0.75
- adapter_router_first: bfloat16 [1024, 64], P('shard'), may hold values from -0.1875 to 0.1875
- adapter_router_second: bfloat16 [64, 32], P(None, 'shard'), may hold values from -0.1875 to 0.1875
- expert_gate_up_weight: bfloat16 [32, 1024, 1024], P('shard'), may hold values from -0.1875 to 0.1875
- expert_down_weight: bfloat16 [32, 512, 1024], P('shard'), may hold values from -1 to 1
- adapter_expert_first: bfloat16 [32, 1024, 128], P('shard'), may hold values from -0.1875 to 0.1875
- adapter_expert_second: bfloat16 [32, 64, 1024], P('shard'), may hold values from -0.75 to 0.75
- adapter_expert_down_first: bfloat16 [32, 512, 64], P('shard'), may hold values from -0.25 to 0.25
- adapter_expert_down_second: bfloat16 [32, 64, 1024], P('shard'), may hold values from -1.5 to 1.5
Outputs:
- block_out: bfloat16 [24576, 1024], P(('rep', 'shard'))
- input_grad: bfloat16 [24576, 1024], P(('rep', 'shard'))
- grad_lora_in_qkv: float32 [1024, 192], P('shard')
- grad_lora_out_qkv: float32 [64, 2048], P(None, 'shard')
- grad_lora_in_out: float32 [1024, 64], P('shard')
- grad_lora_out_out: float32 [64, 1024], P(None, 'shard')
- grad_lora_in_router: float32 [1024, 64], P('shard')
- grad_lora_out_router: float32 [64, 32], P(None, 'shard')
- grad_lora_expert_in: float32 [32, 1024, 128], P('shard')
- grad_lora_expert_mid: float32 [32, 64, 1024], P('shard')
- grad_lora_expert_down_in: float32 [32, 512, 64], P('shard')
- grad_lora_expert_down_out: float32 [32, 64, 1024], P('shard')
The draws below stay inside these ranges and needn't reach their ends.
Inputs may be any that keep to these rules, and one draw needn't show every extreme that they name: `routes`: each row names 8 different experts. Among the rows of one device no expert is named by more than 240 rows, and in some device's rows one expert is named by exactly 240.
All inputs are finite; a program needn't handle non-finite values.
Results may differ from the reference program's by a relative error of at most 0.024.
The reference program's roundings to bfloat16 on the way count: a program that leaves them out, or rounds other values in their place, can miss the bound.
Values may be sent and summed in bfloat16 or wider, within the bound.
A program may use at most 448 MiB of HBM per device.

```python
import math
import jax
import jax.numpy as jnp
import numpy as np
from jax import lax

MODEL_WIDTH = 1024
QUERY_HEADS = 16
KEY_HEADS = 8
HEAD_SIZE = 64
EXPERT_COUNT = 32
EXPERT_HIDDEN = 512
TOPK = 8
ADAPTER_RANK = 16
ADAPTER_POOL = 4
PROMPT = 1024
CONT_LEN = 512
SEQS = 2
GROUP_TOKENS = 1536
GROUPS = 16
TOKENS = 24576
TOK_DEV = 768
CAP = 240
PROJECT_COLUMNS = 2048
N_SHARD = 2


def place_ends(entries, own_key, smallest, largest):
    longest = entries.shape.index(max(entries.shape))
    spots = []
    for shift in (0, 1):
        where = [jax.random.randint(jax.random.fold_in(own_key, axis), (), 0, length) for axis, length in enumerate(entries.shape)]
        where[longest] = (where[longest] + shift) % entries.shape[longest]
        spots.append(tuple(where))
    return entries.at[spots[0]].set(smallest).at[spots[1]].set(largest)


def level_of(key, shape, cuts, least, top_value):
    def one(dim, parts):
        steps = jax.random.uniform(jax.random.fold_in(jax.random.fold_in(key, 6), dim), (parts,), jnp.float32, least / len(cuts), top_value / len(cuts))
        return jnp.repeat(jnp.exp(steps), shape[dim] // parts).reshape((-1,) + (1,) * (len(shape) - dim - 1))

    gain = one(*cuts[0])
    for cut in cuts[1:]:
        gain = gain * one(*cut)
    return gain


def assign_block(own_key, own, number, rows, count, top, bound, skew):
    order = jax.random.permutation(own_key, count)
    packed, ordinary = load_shares(count, rows * top, bound, skew, True), load_shares(count, rows * top, bound, skew, False)
    places = jnp.arange(count)

    def named(sizes, offset_by):
        used = int((sizes > 0).sum())
        fixed = max(1, used // 4)
        moved = fixed + (places - fixed + offset_by * (used - fixed)) % max(1, count - fixed)
        return jnp.zeros((count,), jnp.int32).at[order[jnp.where(places < fixed, places, moved)]].set(jnp.asarray(sizes, jnp.int32))

    sizes = jnp.where(number % 4 == 0, named(packed, number // 4), named(ordinary, number - number // 4 - 1))
    mixed = jax.random.permutation(jax.random.fold_in(own, 3), count)
    source_of, receiver = mixed[0:count // 2 * 2:2], mixed[1:count // 2 * 2:2]
    room = jnp.minimum(sizes[source_of] - 1, bound - sizes[receiver]) // 2
    room = jnp.where((source_of == order[0]) | (receiver == order[0]) | (sizes[receiver] == 0), 0, jnp.maximum(room, 0))
    moved = jax.random.randint(jax.random.fold_in(own, 4), (count // 2,), 0, 1 << 20) % (room + 1)
    sizes = sizes.at[source_of].add(-moved).at[receiver].add(moved)
    members = jnp.searchsorted(jnp.cumsum(sizes), jnp.arange(rows * top), side="right").astype(jnp.int32)
    table = members.reshape(top, rows).T
    table = table[jax.random.permutation(jax.random.fold_in(own, 1), rows)]
    offset_by = jax.random.randint(jax.random.fold_in(own, 2), (rows, 1), 0, top)
    return jnp.take_along_axis(table, (jnp.arange(top)[None, :] + offset_by) % top, axis=1)


def load_shares(count, total, most, slope, full):
    weights = [(1 << 20) // math.isqrt(grade ** slope) + 1 for grade in range(1, count + 1)]
    largest = most if full else min(most, max(-(-total // count), total * weights[0] // sum(weights)))
    least = 1 if total - largest >= count - 1 else 0
    counts, spare = [largest] + [least] * (count - 1), total - largest - least * (count - 1)
    while spare > 0:
        free = [i for i in range(1, count) if counts[i] < largest] or [i for i in range(1, count) if counts[i] < most]
        whole, left = sum([weights[i] for i in free]), spare
        for i in free:
            more = min(most - counts[i], max(1, left * weights[i] // whole), spare)
            counts[i] = counts[i] + more
            spare = spare - more
    return np.array(counts)


def scatter_about(rng, shape, width, bound, cuts=(), held_as=jnp.bfloat16):
    array = width * jax.random.normal(rng, shape, jnp.float32)
    if cuts:
        array = array * level_of(rng, shape, cuts, -0.22, 0.18)
    return jnp.clip(array, -bound, bound).astype(held_as)


def setup_inputs(seed: int = 0) -> dict:
    key_list = jax.random.split(jax.random.key(seed), 22)
    layer_input = scatter_about(key_list[0], (TOKENS, MODEL_WIDTH), 1.0, 6.0, ((0, 32),))
    output_gradient = scatter_about(key_list[1], (TOKENS, MODEL_WIDTH), 1.0, 6.0, ((0, 32),))
    routes_keys = jax.random.split(jax.random.fold_in(key_list[2], 1), TOKENS // TOK_DEV)
    routes_turns = jax.random.permutation(jax.random.fold_in(key_list[2], 3), TOKENS // TOK_DEV)
    routes = jax.vmap(lambda own, number: assign_block(jax.random.fold_in(key_list[2], 2), own, number, TOK_DEV, EXPERT_COUNT, TOPK, CAP, 1))(routes_keys, routes_turns).reshape((TOKENS, TOPK))
    sequence_adapter = place_ends(jax.random.randint(key_list[3], (GROUPS, SEQS), 0, ADAPTER_POOL), jax.random.fold_in(key_list[3], 1), 0, ADAPTER_POOL - 1).astype(jnp.int32)
    attention_gain = jnp.clip(1.0 + 0.18 * jax.random.normal(key_list[4], (MODEL_WIDTH,), jnp.float32), 0.1, 1.9)
    experts_gain = jnp.clip(1.0 + 0.18 * jax.random.normal(key_list[5], (MODEL_WIDTH,), jnp.float32), 0.1, 1.9)
    project_weight = scatter_about(key_list[6], (MODEL_WIDTH, PROJECT_COLUMNS), (MODEL_WIDTH // 2) ** -0.5, 0.25, ((1, 2),))
    output_weight = scatter_about(key_list[7], (QUERY_HEADS * HEAD_SIZE, MODEL_WIDTH), (max(QUERY_HEADS * HEAD_SIZE // 16, 1)) ** -0.5, 0.75, ((0, 2),))
    router_weight = scatter_about(key_list[8], (MODEL_WIDTH, EXPERT_COUNT), (4 * MODEL_WIDTH) ** -0.5, 0.09375, ((0, 2),))
    adapter_project_first = scatter_about(key_list[9], (MODEL_WIDTH, 3 * ADAPTER_POOL * ADAPTER_RANK), MODEL_WIDTH ** -0.5, 0.1875, ((0, 2),))
    adapter_project_second = scatter_about(key_list[10], (ADAPTER_POOL * ADAPTER_RANK, PROJECT_COLUMNS), (4 * ADAPTER_RANK) ** -0.5, 0.75, ((1, 2),))
    adapter_output_first = scatter_about(key_list[11], (QUERY_HEADS * HEAD_SIZE, ADAPTER_POOL * ADAPTER_RANK), (max(QUERY_HEADS * HEAD_SIZE // 16, 1)) ** -0.5, 0.75, ((0, 2),))
    adapter_output_second = scatter_about(key_list[12], (ADAPTER_POOL * ADAPTER_RANK, MODEL_WIDTH), (4 * ADAPTER_RANK) ** -0.5, 0.75, ((1, 2),))
    adapter_router_first = scatter_about(key_list[13], (MODEL_WIDTH, ADAPTER_POOL * ADAPTER_RANK), MODEL_WIDTH ** -0.5, 0.1875, ((0, 2),))
    adapter_router_second = scatter_about(key_list[14], (ADAPTER_POOL * ADAPTER_RANK, EXPERT_COUNT), (64 * ADAPTER_RANK) ** -0.5, 0.1875, ((1, 2),))
    expert_gate_up_weight = scatter_about(key_list[15], (EXPERT_COUNT, MODEL_WIDTH, 2 * EXPERT_HIDDEN), MODEL_WIDTH ** -0.5, 0.1875, ((0, 2),))
    expert_down_weight = scatter_about(key_list[16], (EXPERT_COUNT, EXPERT_HIDDEN, MODEL_WIDTH), (max(EXPERT_HIDDEN // 16, 1)) ** -0.5, 1.0, ((0, 2),))
    adapter_expert_first = scatter_about(key_list[17], (EXPERT_COUNT, MODEL_WIDTH, 2 * ADAPTER_POOL * ADAPTER_RANK), MODEL_WIDTH ** -0.5, 0.1875, ((0, 2),))
    adapter_expert_second = scatter_about(key_list[18], (EXPERT_COUNT, ADAPTER_POOL * ADAPTER_RANK, 2 * EXPERT_HIDDEN), (4 * ADAPTER_RANK) ** -0.5, 0.75, ((0, 2),))
    adapter_expert_down_first = scatter_about(key_list[19], (EXPERT_COUNT, EXPERT_HIDDEN, ADAPTER_POOL * ADAPTER_RANK), EXPERT_HIDDEN ** -0.5, 0.25, ((0, 2),))
    adapter_expert_down_second = scatter_about(key_list[20], (EXPERT_COUNT, ADAPTER_POOL * ADAPTER_RANK, MODEL_WIDTH), ADAPTER_RANK ** -0.5, 1.5, ((0, 2),))
    return dict(layer_input=layer_input, output_gradient=output_gradient, routes=routes, sequence_adapter=sequence_adapter, attention_gain=attention_gain, experts_gain=experts_gain, project_weight=project_weight, output_weight=output_weight, router_weight=router_weight, adapter_project_first=adapter_project_first, adapter_project_second=adapter_project_second, adapter_output_first=adapter_output_first, adapter_output_second=adapter_output_second, adapter_router_first=adapter_router_first, adapter_router_second=adapter_router_second, expert_gate_up_weight=expert_gate_up_weight, expert_down_weight=expert_down_weight, adapter_expert_first=adapter_expert_first, adapter_expert_second=adapter_expert_second, adapter_expert_down_first=adapter_expert_down_first, adapter_expert_down_second=adapter_expert_down_second)


EPSILON = 1e-06
THETA = 10000.0
NEGATIVE = -1e+30
HIGHEST = lax.Precision.HIGHEST

@jax.custom_vjp
def lowrank_apply(v):
    return lax.optimization_barrier(v.astype(jnp.bfloat16)).astype(jnp.float32)

@jax.custom_vjp
def lowrank_backward(v):
    return v

def low_keep(v):
    return (lowrank_apply(v), None)

def low_pass(kept, grad):
    return (grad,)

def back_keep(v):
    return (v, None)

def back_low(kept, grad):
    return (lowrank_apply(grad),)
lowrank_apply.defvjp(low_keep, low_pass)
lowrank_backward.defvjp(back_keep, back_low)

def matrix_product(left_side, right_side):
    return jnp.dot(left_side, right_side, precision=HIGHEST)

def rms_norm(values, gain_row):
    return values * lax.rsqrt(lax.optimization_barrier(jnp.mean(values * values, axis=-1, keepdims=True)) + EPSILON) * gain_row

def adapter_rank_mask(onehot, copies):
    widened = jnp.repeat(onehot, ADAPTER_RANK, axis=-1)
    return jnp.concatenate([widened] * copies, axis=-1)

def token_layout(row_position):
    past_prompt = jnp.maximum(row_position - PROMPT, 0)
    sequence = jnp.where(row_position < PROMPT, 0, 1 + past_prompt // CONT_LEN).astype(jnp.int32)
    position = jnp.where(row_position < PROMPT, row_position, PROMPT + past_prompt % CONT_LEN).astype(jnp.int32)
    return (sequence, position)

def rotary_table(position):
    half_width = HEAD_SIZE // 2
    frequency = jnp.exp(jnp.arange(half_width, dtype=jnp.float32) * (-2.0 * math.log(THETA) / HEAD_SIZE))
    angle_table = position.astype(jnp.float32)[:, None] * frequency[None, :]
    return (jnp.cos(angle_table), jnp.sin(angle_table))

def rotate_halves(values, cosine_table, sine_table):
    half_width = HEAD_SIZE // 2
    first_half = values[..., :half_width]
    second_half = values[..., half_width:]
    cos_heads = cosine_table[:, None, :]
    sin_heads = sine_table[:, None, :]
    return jnp.concatenate([first_half * cos_heads - second_half * sin_heads, second_half * cos_heads + first_half * sin_heads], axis=-1)

def attention(queries, key_row_set, value_row_set, sequence, position):
    block_row_set = min(512, GROUP_TOKENS)
    blocks = GROUP_TOKENS // block_row_set
    score_scale = HEAD_SIZE ** (-0.5)

    def one_block(parts_list):
        query_tile, seq_rows, pos_rows = parts_list
        grouped_apply = query_tile.reshape(block_row_set, KEY_HEADS, QUERY_HEADS // KEY_HEADS, HEAD_SIZE)
        scores = lowrank_backward(jnp.einsum('bkgd,nkd->kgbn', grouped_apply, key_row_set, precision=HIGHEST) * score_scale)
        visible = ((sequence[None, :] == 0) | (sequence[None, :] == seq_rows[:, None])) & (position[None, :] <= pos_rows[:, None])
        scores = jnp.where(visible[None, None], scores, NEGATIVE)
        probs = lowrank_apply(jax.nn.softmax(scores, axis=-1))
        mixed_out = jnp.einsum('kgbn,nkd->bkgd', probs, value_row_set, precision=HIGHEST)
        return mixed_out.reshape(block_row_set, QUERY_HEADS * HEAD_SIZE)
    parts_list = (queries.reshape(blocks, block_row_set, QUERY_HEADS, HEAD_SIZE), sequence.reshape(blocks, block_row_set), position.reshape(blocks, block_row_set))
    return lax.map(jax.checkpoint(one_block), parts_list).reshape(GROUP_TOKENS, QUERY_HEADS * HEAD_SIZE)

def group_pass(inputs, cotangent, route_rows, chosen, frozen, trainable_params):
    attention_gain, experts_gain, project_weight, output_weight, router_weight, expert_gate_up_weight, expert_down_weight = frozen
    adapter_rank_width = ADAPTER_POOL * ADAPTER_RANK
    query_width = QUERY_HEADS * HEAD_SIZE
    key_value_width = KEY_HEADS * HEAD_SIZE
    group_cap = CAP * N_SHARD
    sequence, position = token_layout(jnp.arange(GROUP_TOKENS, dtype=jnp.int32))
    adapter = chosen[sequence]
    onehot = (adapter[:, None] == jnp.arange(ADAPTER_POOL, dtype=jnp.int32)[None, :]).astype(jnp.float32)
    cosine_table, sine_table = rotary_table(position)
    flat_routes = route_rows.reshape(-1)
    route_hits = (flat_routes[:, None] == jnp.arange(EXPERT_COUNT, dtype=jnp.int32)[None, :]).astype(jnp.int32)
    slot_index = lax.optimization_barrier(jnp.sum((jnp.cumsum(route_hits, axis=0) - 1) * route_hits, axis=1))
    target = (flat_routes * group_cap + slot_index).astype(jnp.int32)
    owner_token = jnp.arange(GROUP_TOKENS * TOPK, dtype=jnp.int32) // TOPK
    source = jnp.full((EXPERT_COUNT * group_cap,), GROUP_TOKENS, jnp.int32).at[target].set(owner_token).reshape(EXPERT_COUNT, group_cap)

    def forward(residual, in_qkv, out_qkv, in_out, out_out, in_router, out_router, ex_in, ex_mid, ex_down_in, ex_down_out):
        normed = lowrank_apply(rms_norm(residual, attention_gain))
        rank_qkv = lowrank_backward(lowrank_apply(matrix_product(normed, in_qkv) * adapter_rank_mask(onehot, 3)))
        rank_extra = jnp.concatenate([matrix_product(rank_qkv[:, :adapter_rank_width], out_qkv[:, :query_width]), matrix_product(rank_qkv[:, adapter_rank_width:2 * adapter_rank_width], out_qkv[:, query_width:query_width + key_value_width]), matrix_product(rank_qkv[:, 2 * adapter_rank_width:], out_qkv[:, query_width + key_value_width:])], axis=1)
        projected_rows = lowrank_backward(matrix_product(normed, project_weight) + rank_extra)
        queries = lowrank_apply(rotate_halves(projected_rows[:, :query_width].reshape(GROUP_TOKENS, QUERY_HEADS, HEAD_SIZE), cosine_table, sine_table))
        key_row_set = lowrank_apply(rotate_halves(projected_rows[:, query_width:query_width + key_value_width].reshape(GROUP_TOKENS, KEY_HEADS, HEAD_SIZE), cosine_table, sine_table))
        value_row_set = lowrank_apply(projected_rows[:, query_width + key_value_width:].reshape(GROUP_TOKENS, KEY_HEADS, HEAD_SIZE))
        mixed = lowrank_backward(lowrank_apply(attention(queries, key_row_set, value_row_set, sequence, position)))
        rank_out = lowrank_backward(lowrank_apply(matrix_product(mixed, in_out) * adapter_rank_mask(onehot, 1)))
        branch = lowrank_backward(matrix_product(mixed, output_weight) + matrix_product(rank_out, out_out))
        hidden_one = residual + branch
        moe_in = lowrank_apply(rms_norm(hidden_one, experts_gain))
        rank_router = lowrank_backward(lowrank_apply(matrix_product(moe_in, in_router) * adapter_rank_mask(onehot, 1)))
        logits = lowrank_backward(matrix_product(moe_in, router_weight) + matrix_product(rank_router, out_router))
        picked = jnp.take_along_axis(logits, route_rows, axis=1)
        gate_weights = jax.nn.softmax(picked, axis=1)
        moe_ext = jnp.concatenate([moe_in, jnp.zeros((1, MODEL_WIDTH), jnp.float32)], axis=0)
        tag_ext = jnp.concatenate([onehot, jnp.zeros((1, ADAPTER_POOL), jnp.float32)], axis=0)

        def expert(parts_list):
            row_position, entry_weight, down_weight, adapter_first, adapter_second, adapter_down_first, adapter_down_second = parts_list
            expert_row_set = lowrank_backward(moe_ext[row_position])
            expert_labels = tag_ext[row_position]
            rank_entry = lowrank_backward(lowrank_apply(matrix_product(expert_row_set, adapter_first) * adapter_rank_mask(expert_labels, 2)))
            gate_and_up = lowrank_backward(matrix_product(expert_row_set, entry_weight) + jnp.concatenate([matrix_product(rank_entry[:, :adapter_rank_width], adapter_second[:, :EXPERT_HIDDEN]), matrix_product(rank_entry[:, adapter_rank_width:], adapter_second[:, EXPERT_HIDDEN:])], axis=1))
            hidden_middle = lowrank_apply(jax.nn.silu(gate_and_up[:, :EXPERT_HIDDEN]) * gate_and_up[:, EXPERT_HIDDEN:])
            rank_lower = lowrank_backward(lowrank_apply(matrix_product(hidden_middle, adapter_down_first) * adapter_rank_mask(expert_labels, 1)))
            return lowrank_backward(lowrank_apply(matrix_product(hidden_middle, down_weight) + matrix_product(rank_lower, adapter_down_second)))
        results = lax.map(jax.checkpoint(expert), (source, expert_gate_up_weight, expert_down_weight, ex_in, ex_mid, ex_down_in, ex_down_out))
        chosen_rows = results.reshape(EXPERT_COUNT * group_cap, MODEL_WIDTH)[target].reshape(GROUP_TOKENS, TOPK, MODEL_WIDTH)
        return hidden_one + lax.optimization_barrier(jnp.sum(gate_weights[:, :, None] * chosen_rows, axis=1))
    result, pullback = jax.vjp(forward, inputs, trainable_params[0], trainable_params[1], trainable_params[2], trainable_params[3], trainable_params[4], trainable_params[5], trainable_params[6], trainable_params[7], trainable_params[8], trainable_params[9])
    return (result, pullback(cotangent))

def reference(layer_input, output_gradient, routes, sequence_adapter, attention_gain, experts_gain, project_weight, output_weight, router_weight, adapter_project_first, adapter_project_second, adapter_output_first, adapter_output_second, adapter_router_first, adapter_router_second, expert_gate_up_weight, expert_down_weight, adapter_expert_first, adapter_expert_second, adapter_expert_down_first, adapter_expert_down_second):
    frozen = (attention_gain.astype(jnp.float32), experts_gain.astype(jnp.float32), project_weight.astype(jnp.float32), output_weight.astype(jnp.float32), router_weight.astype(jnp.float32), expert_gate_up_weight.astype(jnp.float32), expert_down_weight.astype(jnp.float32))
    trainable_params = (adapter_project_first.astype(jnp.float32), adapter_project_second.astype(jnp.float32), adapter_output_first.astype(jnp.float32), adapter_output_second.astype(jnp.float32), adapter_router_first.astype(jnp.float32), adapter_router_second.astype(jnp.float32), adapter_expert_first.astype(jnp.float32), adapter_expert_second.astype(jnp.float32), adapter_expert_down_first.astype(jnp.float32), adapter_expert_down_second.astype(jnp.float32))

    def group_step(totals, parts_list):
        inputs, cotangent, route_rows, chosen = parts_list
        result, grads = group_pass(inputs.astype(jnp.float32), cotangent.astype(jnp.float32), route_rows, chosen, frozen, trainable_params)
        new_totals = tuple((total_part + grad_part for total_part, grad_part in zip(totals, grads[1:])))
        return (new_totals, (result.astype(jnp.bfloat16), grads[0].astype(jnp.bfloat16)))
    start = tuple((jnp.zeros_like(item) for item in trainable_params))
    parts_list = (layer_input.reshape(GROUPS, GROUP_TOKENS, MODEL_WIDTH), output_gradient.reshape(GROUPS, GROUP_TOKENS, MODEL_WIDTH), routes.reshape(GROUPS, GROUP_TOKENS, TOPK), sequence_adapter)
    totals, stacked = lax.scan(group_step, start, parts_list)
    outs_all, grads_all = stacked
    return (outs_all.reshape(TOKENS, MODEL_WIDTH), grads_all.reshape(TOKENS, MODEL_WIDTH), totals[0], totals[1], totals[2], totals[3], totals[4], totals[5], totals[6], totals[7], totals[8], totals[9])
```

```python
import functools
import math

import jax
import jax.numpy as jnp
from jax import lax
from jax.experimental import pallas as pl
from jax.experimental.pallas import tpu as pltpu
from jax.sharding import PartitionSpec as P

MODEL_WIDTH = 1024
QUERY_HEADS = 16
KEY_HEADS = 8
HEAD_SIZE = 64
EXPERT_COUNT = 32
EXPERT_HIDDEN = 512
TOPK = 8
ADAPTER_RANK = 16
ADAPTER_POOL = 4
PROMPT = 1024
CONT_LEN = 512


EPSILON = 1e-06
THETA = 10000.0
NEGATIVE = -1e30
F32, BF16 = jnp.float32, jnp.bfloat16


def dot_nn(a, b):
    return lax.dot_general(a, b, (((1,), (0,)), ((), ())), preferred_element_type=F32)


def dot_nt(a, b):
    return lax.dot_general(a, b, (((1,), (1,)), ((), ())), preferred_element_type=F32)


def dot_tn(a, b):
    return lax.dot_general(a, b, (((0,), (0,)), ((), ())), preferred_element_type=F32)


def expert_kernel(
    carry_acc, carry_grad,
    rows_ref, grad_ref, slot_ref, gate_ref, label_ref,
    entry_ref, down_ref, first_ref, second_ref, down_first_ref, down_second_ref,
    *refs,
):
    refs = list(refs)
    if carry_acc:
        out_in, back_in = refs[0], refs[1]
        refs = refs[2:]
    if carry_grad:
        lora_in = refs[0]
        refs = refs[1:]
    out_ref, back_ref, dgate_ref, lora_ref = refs[:4]
    x_s, dy_s, hid_s, fg_s, fu_s, dgu_s, out_s, back_s, yg_s, dx_s = refs[4:]
    cap = x_s.shape[0]
    tokens = rows_ref.shape[0]
    width = rows_ref.shape[1]
    hidden = down_ref.shape[1]
    rank = ADAPTER_POOL * ADAPTER_RANK
    e = pl.program_id(1)

    @pl.when(e == 0)
    def _():
        if carry_acc:
            out_s[...] = out_in[...]
            back_s[...] = back_in[...]
        else:
            out_s[...] = jnp.zeros_like(out_s)
            back_s[...] = jnp.zeros_like(back_s)

    slots = slot_ref[0, 0]
    gates = gate_ref[0, 0]
    hit = slots == lax.broadcasted_iota(jnp.int32, (cap, tokens), 0)
    pick32 = hit.astype(F32)
    pick = pick32.astype(BF16)
    gate_col = jnp.sum(pick32 * gates, axis=1, keepdims=True)
    label_col = jnp.sum(pick32 * label_ref[0], axis=1, keepdims=True)
    lane = lax.broadcasted_iota(jnp.int32, (cap, 2 * rank), 1)
    lane_label = ((lane // ADAPTER_RANK) % ADAPTER_POOL).astype(F32)
    mask2 = (lane_label == label_col).astype(F32)
    mask1 = mask2[:, :rank]

    x_s[...] = dot_nn(pick, rows_ref[...]).astype(BF16)
    x = x_s[...]
    ue = (dot_nn(x, first_ref[0]) * mask2).astype(BF16)
    ue0, ue1 = ue[:, :rank], ue[:, rank:]
    step = 256
    for n in range(0, hidden, step):
        g = dot_nn(x, entry_ref[0, :, n : n + step]) + dot_nn(ue0, second_ref[0, :, n : n + step])
        u = dot_nn(x, entry_ref[0, :, hidden + n : hidden + n + step]) + dot_nn(
            ue1, second_ref[0, :, hidden + n : hidden + n + step]
        )
        sig = 1.0 / (1.0 + jnp.exp(-g))
        silu = g * sig
        hid_s[:, n : n + step] = (silu * u).astype(BF16)
        fg_s[:, n : n + step] = u * sig * (1.0 + g * (1.0 - sig))
        fu_s[:, n : n + step] = silu
    hid = hid_s[...]
    ud = (dot_nn(hid, down_first_ref[0]) * mask1).astype(BF16)
    dcol = jnp.zeros((cap, 1), F32)
    for n in range(0, width, step):
        cols = slice(n, n + step)
        y = (dot_nn(hid, down_ref[0, :, cols]) + dot_nn(ud, down_second_ref[0, :, cols])).astype(BF16)
        y32 = y.astype(F32)
        gy = dot_nn(pick, grad_ref[:, cols])
        dcol = dcol + jnp.sum(gy * y32, axis=1, keepdims=True)
        dy_s[:, cols] = (gate_col * gy).astype(BF16)
        yg_s[:, cols] = (gate_col * y32).astype(BF16)
    dgate_ref[0, 0] = jnp.sum(pick32 * dcol, axis=0, keepdims=True)
    dy = dy_s[...]
    dud = (dot_nt(dy, down_second_ref[0]) * mask1).astype(BF16)
    for n in range(0, hidden, step):
        dh = dot_nt(dy, down_ref[0, n : n + step, :]) + dot_nt(dud, down_first_ref[0, n : n + step, :])
        dgu_s[:, n : n + step] = (dh * fg_s[:, n : n + step]).astype(BF16)
        dgu_s[:, hidden + n : hidden + n + step] = (dh * fu_s[:, n : n + step]).astype(BF16)
    dgu = dgu_s[...]
    dg, du = dgu[:, :hidden], dgu[:, hidden:]
    due = (
        jnp.concatenate(
            [dot_nt(dg, second_ref[0, :, :hidden]), dot_nt(du, second_ref[0, :, hidden:])], axis=1
        )
        * mask2
    ).astype(BF16)
    for n in range(0, width, step):
        cols = slice(n, n + step)
        dx = dot_nt(dgu, entry_ref[0, cols, :]) + dot_nt(due, first_ref[0, cols, :])
        dx_s[:, cols] = dx.astype(BF16)
    for n in range(0, width, step):
        cols = slice(n, n + step)
        out_s[:, cols] += dot_tn(pick, yg_s[:, cols])
        back_s[:, cols] += dot_tn(pick, dx_s[:, cols])

    def put(lo, hi, val, cols=slice(None)):
        if carry_grad:
            val = val + lora_in[0, lo:hi, cols]
        lora_ref[0, lo:hi, cols] = val.astype(lora_ref.dtype)

    put(0, 2 * rank, dot_tn(due, x))
    put(2 * rank, 3 * rank, dot_tn(ue0, dg), slice(0, hidden))
    put(2 * rank, 3 * rank, dot_tn(ue1, du), slice(hidden, 2 * hidden))
    put(3 * rank, 4 * rank, dot_tn(ud, dy))
    down_t = dot_tn(dud, hid)
    half = rank // 2
    put(4 * rank, 4 * rank + half, down_t[:half], slice(0, hidden))
    put(4 * rank, 4 * rank + half, down_t[half:], slice(hidden, 2 * hidden))

    @pl.when(e == pl.num_programs(1) - 1)
    def _():
        out_ref[...] = out_s[...].astype(out_ref.dtype)
        back_ref[...] = back_s[...].astype(back_ref.dtype)


def experts(rows, grads, slots, gates, labels, weights, cap, first, count, acc=None, lora=None, acc_type=F32, lora_type=F32):
    entry, down, a_first, a_second, d_first, d_second = weights
    blocks = slots.shape[0]
    tokens, width = rows.shape[0] // blocks, rows.shape[1]
    hidden = down.shape[1]
    rank = ADAPTER_POOL * ADAPTER_RANK
    pack = 4 * rank + rank // 2
    at_block = lambda b, e: (b, 0)
    at_expert = lambda b, e: (first + e, 0, 0)
    per = lambda b, e: (b, first + e, 0, 0)
    in_specs = [
        pl.BlockSpec((tokens, width), at_block),
        pl.BlockSpec((tokens, width), at_block),
        pl.BlockSpec((1, 1, 1, tokens), per),
        pl.BlockSpec((1, 1, 1, tokens), per),
        pl.BlockSpec((1, 1, tokens), lambda b, e: (b, 0, 0)),
    ] + [pl.BlockSpec((1,) + w.shape[1:], at_expert) for w in weights]
    args = [rows, grads, slots, gates, labels, *weights]
    if acc is not None:
        in_specs += [pl.BlockSpec((tokens, width), at_block)] * 2
        args += list(acc)
    if lora is not None:
        in_specs += [pl.BlockSpec((1, pack, width), lambda b, e: (b * count + e, 0, 0))]
        args += [lora]
    macs = cap * (width * 2 * hidden * 2 + hidden * width * 2 + 3 * (3 * width * 2 * rank)) + 4 * cap * tokens * width
    return pl.pallas_call(
        functools.partial(expert_kernel, acc is not None, lora is not None),
        grid=(blocks, count),
        in_specs=in_specs,
        out_specs=[
            pl.BlockSpec((tokens, width), at_block),
            pl.BlockSpec((tokens, width), at_block),
            pl.BlockSpec((1, 1, 1, tokens), lambda b, e: (b, e, 0, 0)),
            pl.BlockSpec((1, pack, width), lambda b, e: (b * count + e, 0, 0)),
        ],
        out_shape=[
            jax.ShapeDtypeStruct(rows.shape, acc_type),
            jax.ShapeDtypeStruct(rows.shape, acc_type),
            jax.ShapeDtypeStruct((blocks, count, 1, tokens), F32),
            jax.ShapeDtypeStruct((blocks * count, pack, width), lora_type),
        ],
        scratch_shapes=[
            pltpu.VMEM((cap, width), BF16),
            pltpu.VMEM((cap, width), BF16),
            pltpu.VMEM((cap, hidden), BF16),
            pltpu.VMEM((cap, hidden), F32),
            pltpu.VMEM((cap, hidden), F32),
            pltpu.VMEM((cap, 2 * hidden), BF16),
            pltpu.VMEM((tokens, width), F32),
            pltpu.VMEM((tokens, width), F32),
            pltpu.VMEM((cap, width), BF16),
            pltpu.VMEM((cap, width), BF16),
        ],
        compiler_params=pltpu.CompilerParams(vmem_limit_bytes=58 * 1024 * 1024),
        cost_estimate=pl.CostEstimate(
            flops=2 * macs * blocks * count, transcendentals=cap * hidden * blocks * count,
            bytes_accessed=blocks * count * 4_000_000,
        ),
        name="experts",
    )(*args)


def split_heads(pair, low):
    zero = jnp.zeros_like(pair)
    return jnp.concatenate([jnp.where(low, pair, zero), jnp.where(low, zero, pair)], axis=0)


def attend_kernel(tile, place_ref, q_ref, k_ref, v_ref, pk_ref, pv_ref, o_ref, total_ref):
    tokens = q_ref.shape[0]
    before = pk_ref.shape[0]
    place = place_ref[0]
    low = lax.broadcasted_iota(jnp.int32, (tile, 128), 1) < 64

    def tile_out(i, with_prior):
        q2 = split_heads(q_ref[i * tile : (i + 1) * tile, :], low)
        keys = (i + 1) * tile
        own = dot_nt(q2, k_ref[:keys, :])
        row = lax.broadcasted_iota(jnp.int32, (2 * tile, tile), 0) % tile
        col = lax.broadcasted_iota(jnp.int32, (2 * tile, tile), 1)
        diag = jnp.where(col <= row, own[:, i * tile :], NEGATIVE)
        parts = [diag] if i == 0 else [own[:, : i * tile], diag]
        vals = [v_ref[i * tile : keys, :]] if i == 0 else [v_ref[: i * tile, :], v_ref[i * tile : keys, :]]
        if with_prior:
            prior = dot_nt(q2, pk_ref[...])
            if before > tokens:
                seen = lax.broadcasted_iota(jnp.int32, (2 * tile, before), 1) < place * tokens
                prior = jnp.where(seen, prior, NEGATIVE)
            parts.append(prior)
            vals.append(pv_ref[...])
        peak = functools.reduce(jnp.maximum, [jnp.max(p, axis=1, keepdims=True) for p in parts])
        total = jnp.zeros((2 * tile, 1), F32)
        mix = jnp.zeros((2 * tile, 128), F32)
        for p, v in zip(parts, vals):
            w = jnp.exp(p - peak)
            total = total + jnp.sum(w, axis=1, keepdims=True)
            mix = mix + dot_nn(w.astype(BF16), v)
        mix = mix / total
        o_ref[i * tile : (i + 1) * tile, :] = jnp.where(low, mix[:tile], mix[tile:]).astype(BF16)
        logs = jnp.broadcast_to(peak + jnp.log(total), (2 * tile, 128)).T
        total_ref[0, 0:1, i * tile : (i + 1) * tile] = logs[0:1, :tile]
        total_ref[0, 1:2, i * tile : (i + 1) * tile] = logs[0:1, tile:]

    for i in range(tokens // tile):
        @pl.when(place > 0)
        def _():
            tile_out(i, True)

        @pl.when(place == 0)
        def _():
            tile_out(i, False)


def attend(place, q, kd, vd, pkd, pvd, tile):
    tokens, width = q.shape
    before = pkd.shape[0]
    pairs = width // 128
    at = lambda n, p: (0, n)
    return pl.pallas_call(
        functools.partial(attend_kernel, tile),
        grid_spec=pltpu.PrefetchScalarGridSpec(
            num_scalar_prefetch=1,
            grid=(pairs,),
            in_specs=[pl.BlockSpec((tokens, 128), at)] * 3 + [pl.BlockSpec((before, 128), at)] * 2,
            out_specs=[
                pl.BlockSpec((tokens, 128), at),
                pl.BlockSpec((1, 2, tokens), lambda n, p: (n, 0, 0)),
            ],
        ),
        out_shape=[
            jax.ShapeDtypeStruct((tokens, width), BF16),
            jax.ShapeDtypeStruct((pairs, 2, tokens), F32),
        ],
        compiler_params=pltpu.CompilerParams(vmem_limit_bytes=48 * 1024 * 1024),
        cost_estimate=pl.CostEstimate(
            flops=4 * width * tokens * (tokens + before) * 2, transcendentals=0, bytes_accessed=8 * tokens * width
        ),
        name="attend",
    )(place, q, kd, vd, pkd, pvd)


def attend_back_kernel(
    tile, place_ref, q_ref, do_ref, total_ref, delta_ref, k_ref, v_ref, pk_ref, pv_ref,
    dq_ref, dk_ref, dv_ref, dpk_ref, dpv_ref, dk_s, dv_s, dpk_s, dpv_s, dq_s,
):
    tokens = q_ref.shape[0]
    before = pk_ref.shape[0]
    place = place_ref[0]
    tiles = tokens // tile
    low = lax.broadcasted_iota(jnp.int32, (tile, 128), 1) < 64
    dk_s[...] = jnp.zeros_like(dk_s)
    dv_s[...] = jnp.zeros_like(dv_s)
    dpk_s[...] = jnp.zeros_like(dpk_s)
    dpv_s[...] = jnp.zeros_like(dpv_s)

    def block(q2, do2, logs, delta, k, v, seen, dk_acc, dv_acc, rows, first):
        s = dot_nt(k, q2)
        if seen is not None:
            s = jnp.where(seen, s, NEGATIVE)
        p = jnp.exp(s - logs)
        dp = dot_nt(v, do2)
        ds = (p * (dp - delta)).astype(BF16)
        dv_acc[rows, :] += dot_nn(p.astype(BF16), do2)
        dk_acc[rows, :] += dot_nn(ds, q2)
        dq = dot_tn(ds, k)
        if first:
            dq_s[...] = dq
        else:
            dq_s[...] += dq

    for i in range(tiles):
        here = slice(i * tile, (i + 1) * tile)
        q2 = split_heads(q_ref[here, :], low)
        do2 = split_heads(do_ref[here, :], low)
        logs = jnp.concatenate([total_ref[0, 0:1, here], total_ref[0, 1:2, here]], axis=1)
        delta = jnp.concatenate([delta_ref[0, 0:1, here], delta_ref[0, 1:2, here]], axis=1)
        row = lax.broadcasted_iota(jnp.int32, (tile, 2 * tile), 1) % tile
        col = lax.broadcasted_iota(jnp.int32, (tile, 2 * tile), 0)
        for j in range(i + 1):
            keys = slice(j * tile, (j + 1) * tile)
            block(q2, do2, logs, delta, k_ref[keys, :], v_ref[keys, :], col <= row if j == i else None, dk_s, dv_s, keys, j == 0)

        @pl.when(place > 0)
        def _():
            for j in range(before // tile):
                keys = slice(j * tile, (j + 1) * tile)
                seen = None
                if before > tokens:
                    seen = (lax.broadcasted_iota(jnp.int32, (tile, 2 * tile), 0) + j * tile) < place * tokens
                block(q2, do2, logs, delta, pk_ref[keys, :], pv_ref[keys, :], seen, dpk_s, dpv_s, keys, False)

        dq = dq_s[...]
        dq_ref[here, :] = jnp.where(low, dq[:tile], dq[tile:])

    dk_ref[...] = dk_s[...]
    dv_ref[...] = dv_s[...]
    dpk_ref[...] = dpk_s[...]
    dpv_ref[...] = dpv_s[...]


def attend_back(place, q, do, total, delta, kd, vd, pkd, pvd, tile):
    tokens, width = q.shape
    before = pkd.shape[0]
    pairs = width // 128
    at = lambda n, p: (0, n)
    row = lambda n, p: (n, 0, 0)
    return pl.pallas_call(
        functools.partial(attend_back_kernel, tile),
        grid_spec=pltpu.PrefetchScalarGridSpec(
            num_scalar_prefetch=1,
            grid=(pairs,),
            in_specs=[pl.BlockSpec((tokens, 128), at)] * 2
            + [pl.BlockSpec((1, 2, tokens), row)] * 2
            + [pl.BlockSpec((tokens, 128), at)] * 2
            + [pl.BlockSpec((before, 128), at)] * 2,
            out_specs=[pl.BlockSpec((tokens, 128), at)] * 3 + [pl.BlockSpec((before, 128), at)] * 2,
            scratch_shapes=[
                pltpu.VMEM((tokens, 128), F32),
                pltpu.VMEM((tokens, 128), F32),
                pltpu.VMEM((before, 128), F32),
                pltpu.VMEM((before, 128), F32),
                pltpu.VMEM((2 * tile, 128), F32),
            ],
        ),
        out_shape=[jax.ShapeDtypeStruct((tokens, width), F32)] * 3
        + [jax.ShapeDtypeStruct((before, width), F32)] * 2,
        compiler_params=pltpu.CompilerParams(vmem_limit_bytes=48 * 1024 * 1024),
        cost_estimate=pl.CostEstimate(
            flops=10 * width * tokens * (tokens + before) * 2, transcendentals=0, bytes_accessed=24 * tokens * width
        ),
        name="attend_back",
    )(place, q, do, total, delta, kd, vd, pkd, pvd)


def rank_mask(onehot, copies):
    widened = jnp.repeat(onehot, ADAPTER_RANK, axis=-1)
    return jnp.concatenate([widened] * copies, axis=-1)


def token_layout(row_position):
    past_prompt = jnp.maximum(row_position - PROMPT, 0)
    sequence = jnp.where(row_position < PROMPT, 0, 1 + past_prompt // CONT_LEN)
    position = jnp.where(row_position < PROMPT, row_position, PROMPT + past_prompt % CONT_LEN)
    return (sequence, position)


def rotary_table(position):
    half_width = HEAD_SIZE // 2
    frequency = jnp.exp(
        jnp.arange(half_width, dtype=jnp.float32) * (-2.0 * math.log(THETA) / HEAD_SIZE)
    )
    angle_table = position.astype(jnp.float32)[:, None] * frequency[None, :]
    return (jnp.cos(angle_table), jnp.sin(angle_table))


def rotate_halves(values, cosine_table, sine_table):
    half_width = HEAD_SIZE // 2
    first_half = values[..., :half_width]
    second_half = values[..., half_width:]
    cos_heads = cosine_table[:, None, :]
    sin_heads = sine_table[:, None, :]
    return jnp.concatenate(
        [
            first_half * cos_heads - second_half * sin_heads,
            second_half * cos_heads + first_half * sin_heads,
        ],
        axis=-1,
    )


def norm_back(grad_in, values, inverse, gain_row):
    scaled = grad_in * gain_row
    normed = values * inverse
    return inverse * (scaled - normed * jnp.mean(scaled * normed, axis=-1, keepdims=True))


def twice(x):
    rows = x.shape[0]
    return jnp.repeat(x.reshape(rows, KEY_HEADS, 1, HEAD_SIZE), 2, axis=2).reshape(rows, -1)


def fold(x):
    rows = x.shape[0]
    return x.reshape(rows, KEY_HEADS, 2, HEAD_SIZE).sum(axis=2).reshape(rows, -1)


def slot_rows(hit):
    tokens = hit.shape[1]
    before = (
        jnp.arange(tokens, dtype=jnp.int32)[:, None] < jnp.arange(tokens, dtype=jnp.int32)[None, :]
    ).astype(BF16)
    rank = dot_nn(hit.astype(BF16), before)
    return jnp.where(hit, rank.astype(jnp.int32), -1)


def swap(x):
    return lax.ppermute(x, "shard", [(0, 1), (1, 0)])


def local(
    layer_input,
    output_gradient,
    routes,
    sequence_adapter,
    attention_gain,
    experts_gain,
    project_weight,
    output_weight,
    router_weight,
    adapter_project_first,
    adapter_project_second,
    adapter_output_first,
    adapter_output_second,
    adapter_router_first,
    adapter_router_second,
    expert_gate_up_weight,
    expert_down_weight,
    adapter_expert_first,
    adapter_expert_second,
    adapter_expert_down_first,
    adapter_expert_down_second,
):
    shards = lax.axis_size("shard")
    me = lax.axis_index("shard")
    tokens = layer_input.shape[0]
    owned = expert_gate_up_weight.shape[0]
    rank = ADAPTER_POOL * ADAPTER_RANK
    qw = QUERY_HEADS * HEAD_SIZE
    kw = KEY_HEADS * HEAD_SIZE
    cap = tokens * TOPK // EXPERT_COUNT * 5 // 4
    cap = -(-cap // 16) * 16
    tile = min(256, tokens)
    scale = HEAD_SIZE ** (-0.5)
    pair = shards == 2

    project = lax.all_gather(project_weight, "shard", axis=1, tiled=True)
    firsts = lax.all_gather(
        jnp.concatenate(
            [adapter_project_first, adapter_output_first, adapter_router_first, router_weight], axis=1
        ),
        "shard", axis=0, tiled=True,
    )
    a_qkv, a_out, a_router, w_router = (
        firsts[:, : 3 * rank],
        firsts[:, 3 * rank : 4 * rank],
        firsts[:, 4 * rank : 5 * rank],
        firsts[:, 5 * rank :],
    )
    seconds = lax.all_gather(
        jnp.concatenate([adapter_project_second, adapter_output_second, adapter_router_second], axis=1),
        "shard", axis=0, tiled=False,
    )

    def columns(lo, width):
        return seconds[:, :, lo : lo + width].transpose(1, 0, 2).reshape(rank, shards * width)

    pw, ow, rw = adapter_project_second.shape[1], adapter_output_second.shape[1], adapter_router_second.shape[1]
    b_qkv, b_out, b_router = columns(0, pw), columns(pw, ow), columns(pw + ow, rw)
    w_out = lax.all_gather(output_weight, "shard", axis=0, tiled=True)

    local_rows = me * tokens + jnp.arange(tokens, dtype=jnp.int32)
    sequence, position = token_layout(local_rows)

    def adapters_of(seq):
        return jnp.sum(
            jnp.where(
                seq[:, None] == jnp.arange(sequence_adapter.shape[1], dtype=jnp.int32)[None, :],
                sequence_adapter,
                0,
            ),
            axis=1,
        )

    adapter = adapters_of(sequence)
    onehot = (adapter[:, None] == jnp.arange(ADAPTER_POOL, dtype=jnp.int32)[None, :]).astype(BF16)
    mask_one = rank_mask(onehot, 1)
    mask_three = rank_mask(onehot, 3)
    cosine_table, sine_table = rotary_table(position)

    if pair:
        blocks_routes = [routes, swap(routes)]
        other_rows = (1 - me) * tokens + jnp.arange(tokens, dtype=jnp.int32)
        labels = [adapter, adapters_of(token_layout(other_rows)[0])]
        grads_other = swap(output_gradient)
    else:
        everyone = lax.all_gather(routes, "shard", axis=0, tiled=False)
        blocks_routes = [everyone[j] for j in range(shards)]
        whole = adapters_of(token_layout(jnp.arange(shards * tokens, dtype=jnp.int32))[0])
        labels = [whole[j * tokens : (j + 1) * tokens] for j in range(shards)]
    mine = me * owned + jnp.arange(owned, dtype=jnp.int32)
    slots = [
        slot_rows(jnp.any(r.T[None, :, :] == mine[:, None, None], axis=1)).reshape(1, owned, 1, tokens)
        for r in blocks_routes
    ]
    labels = [l.astype(F32).reshape(1, 1, tokens) for l in labels]
    chosen = jnp.any(routes[:, :, None] == jnp.arange(EXPERT_COUNT, dtype=jnp.int32), axis=1)

    residual = layer_input.astype(F32)
    inverse_one = lax.rsqrt(jnp.mean(residual * residual, axis=-1, keepdims=True) + EPSILON)
    normed = (residual * inverse_one * attention_gain).astype(BF16)
    rank_qkv = (dot_nn(normed, a_qkv) * mask_three).astype(BF16)
    extra = jnp.concatenate(
        [
            dot_nn(rank_qkv[:, :rank], b_qkv[:, :qw]),
            dot_nn(rank_qkv[:, rank : 2 * rank], b_qkv[:, qw : qw + kw]),
            dot_nn(rank_qkv[:, 2 * rank :], b_qkv[:, qw + kw :]),
        ],
        axis=1,
    )
    pre = dot_nn(normed, project) + extra
    queries = (
        rotate_halves(pre[:, :qw].reshape(tokens, QUERY_HEADS, HEAD_SIZE), cosine_table, sine_table)
        .astype(BF16)
        .reshape(tokens, qw)
        * jnp.bfloat16(scale)
    )
    keys = (
        rotate_halves(pre[:, qw : qw + kw].reshape(tokens, KEY_HEADS, HEAD_SIZE), cosine_table, sine_table)
        .astype(BF16)
        .reshape(tokens, kw)
    )
    values = pre[:, qw + kw :].astype(BF16)
    keyval = jnp.concatenate([keys, values], axis=1)
    if pair:
        prior = lax.ppermute(keyval, "shard", [(0, 1)])
    else:
        prior = lax.all_gather(keyval, "shard", axis=0, tiled=True)
    key2, value2 = twice(keys), twice(values)
    prior_key2, prior_value2 = twice(prior[:, :kw]), twice(prior[:, kw:])
    place = me.astype(jnp.int32).reshape(1)
    mixed, log_total = attend(place, queries, key2, value2, prior_key2, prior_value2, tile)

    rank_out = (dot_nn(mixed, a_out) * mask_one).astype(BF16)
    hidden_one = residual + dot_nn(mixed, w_out) + dot_nn(rank_out, b_out)
    inverse_two = lax.rsqrt(jnp.mean(hidden_one * hidden_one, axis=-1, keepdims=True) + EPSILON)
    moe_in = (hidden_one * inverse_two * experts_gain).astype(BF16)
    rank_router = (dot_nn(moe_in, a_router) * mask_one).astype(BF16)
    logits = dot_nn(moe_in, w_router) + dot_nn(rank_router, b_router)
    peak = jnp.max(jnp.where(chosen, logits, -jnp.inf), axis=1, keepdims=True)
    weights = jnp.where(chosen, jnp.exp(jnp.where(chosen, logits, peak) - peak), 0.0)
    gates = weights / jnp.sum(weights, axis=1, keepdims=True)
    gates_t = gates.T
    grad_top = output_gradient.astype(F32)
    experts_weights = (
        expert_gate_up_weight,
        expert_down_weight,
        adapter_expert_first,
        adapter_expert_second,
        adapter_expert_down_first,
        adapter_expert_down_second,
    )
    if pair:
        half = owned // 2
        shape = (1, owned, 1, tokens)
        rows_other = swap(moe_in)
        gates_own = lax.dynamic_slice_in_dim(gates_t, me * owned, owned, 0).reshape(shape)
        gates_other = swap(lax.dynamic_slice_in_dim(gates_t, (1 - me) * owned, owned, 0)).reshape(shape)
        own = (moe_in, output_gradient, slots[0], gates_own, labels[0], experts_weights, cap)
        other = (rows_other, grads_other, slots[1], gates_other, labels[1], experts_weights, cap)
        out_a, back_a, dg_a, lora_a = experts(*own, 0, half)
        out_b, back_b, dg_b, lora_low = experts(*other, 0, half, lora=lora_a, lora_type=BF16)
        out_c, back_c, dg_c, lora_c = experts(*other, half, half, acc=(out_b, back_b), acc_type=BF16)
        out_own, back_own, dg_d, lora_high = experts(
            *own, half, half, acc=(out_a, back_a), lora=lora_c, lora_type=BF16
        )
        back_got, dg_got = swap(back_c), swap(jnp.concatenate([dg_b, dg_c], axis=1))
        out_got = swap(out_c)
        combined = out_own + out_got.astype(F32)
        grad_moe = back_own + back_got.astype(F32)
        dg_own = jnp.concatenate([dg_a, dg_d], axis=1).reshape(owned, tokens)
        dg_got = dg_got.reshape(owned, tokens)
        dg_t = jnp.concatenate(
            [jnp.where(me == 0, dg_own, dg_got), jnp.where(me == 0, dg_got, dg_own)], axis=0
        )
        low_total = lax.psum(lora_low, "rep")
        lora_high, low_total = lax.optimization_barrier((lora_high, low_total))
        lora_total = jnp.concatenate([low_total, lax.psum(lora_high, "rep")], axis=0)
    else:
        rows_all = lax.all_gather(moe_in, "shard", axis=0, tiled=True)
        grads_all = lax.all_gather(output_gradient, "shard", axis=0, tiled=True)
        gates_all = lax.dynamic_slice_in_dim(
            lax.all_gather(gates_t, "shard", axis=0, tiled=False), me * owned, owned, 1
        ).reshape(shards, owned, 1, tokens)
        out_p, back_p, dg_p, lora_p = experts(
            rows_all, grads_all, jnp.concatenate(slots, axis=0), gates_all, jnp.concatenate(labels, axis=0),
            experts_weights, cap, 0, owned, acc_type=BF16,
        )
        combined = lax.psum_scatter(out_p, "shard", scatter_dimension=0, tiled=True).astype(F32)
        grad_moe = lax.psum_scatter(back_p, "shard", scatter_dimension=0, tiled=True).astype(F32)
        dg_all = lax.all_gather(dg_p.reshape(shards, owned, tokens), "shard", axis=0, tiled=False)
        dg_t = lax.dynamic_index_in_dim(dg_all, me, 1, keepdims=False).reshape(EXPERT_COUNT, tokens)
        lora_total = lax.psum(
            lora_p.reshape((shards, owned) + lora_p.shape[1:]).sum(axis=0).astype(BF16), "rep"
        )
    block_out = (hidden_one + combined).astype(BF16)

    dgates = dg_t.T
    dpicked = gates * (dgates - jnp.sum(dgates * gates, axis=-1, keepdims=True))
    grad_logits = dpicked.astype(BF16)
    grad_out_router = dot_tn(rank_router, grad_logits)
    grad_rank_router = dot_nt(grad_logits, b_router).astype(BF16) * mask_one
    grad_in_router = dot_tn(moe_in, grad_rank_router)
    grad_moe = grad_moe + dot_nt(grad_logits, w_router) + dot_nt(grad_rank_router, a_router)
    grad_hidden = grad_top + norm_back(grad_moe, hidden_one, inverse_two, experts_gain)
    grad_branch = grad_hidden.astype(BF16)
    grad_out_out = dot_tn(rank_out, grad_branch)
    grad_rank_out = dot_nt(grad_branch, b_out).astype(BF16) * mask_one
    grad_in_out = dot_tn(mixed, grad_rank_out)
    grad_mixed = (dot_nt(grad_branch, w_out) + dot_nt(grad_rank_out, a_out)).astype(BF16)
    delta = (
        (mixed.astype(F32) * grad_mixed.astype(F32))
        .reshape(tokens, KEY_HEADS, 2, HEAD_SIZE)
        .sum(axis=-1)
        .transpose(1, 2, 0)
    )
    dq, dk2, dv2, dpk2, dpv2 = attend_back(
        place, queries, grad_mixed, log_total, delta, key2, value2, prior_key2, prior_value2, tile
    )
    sent = jnp.concatenate([fold(dpk2), fold(dpv2)], axis=1).astype(BF16)
    if pair:
        got = lax.ppermute(sent, "shard", [(1, 0)]).astype(F32)
    else:
        got = lax.psum_scatter(sent, "shard", scatter_dimension=0, tiled=True).astype(F32)
    dk = fold(dk2) + got[:, :kw]
    dv = fold(dv2) + got[:, kw:]
    dq_pre = rotate_halves(
        (dq * scale).reshape(tokens, QUERY_HEADS, HEAD_SIZE), cosine_table, -sine_table
    ).reshape(tokens, qw)
    dk_pre = rotate_halves(
        dk.reshape(tokens, KEY_HEADS, HEAD_SIZE), cosine_table, -sine_table
    ).reshape(tokens, kw)
    grad_pre = jnp.concatenate([dq_pre, dk_pre, dv], axis=1).astype(BF16)
    gq, gk, gv = grad_pre[:, :qw], grad_pre[:, qw : qw + kw], grad_pre[:, qw + kw :]
    grad_out_qkv = jnp.concatenate(
        [
            dot_tn(rank_qkv[:, :rank], gq),
            dot_tn(rank_qkv[:, rank : 2 * rank], gk),
            dot_tn(rank_qkv[:, 2 * rank :], gv),
        ],
        axis=1,
    )
    grad_rank_qkv = (
        jnp.concatenate(
            [
                dot_nt(gq, b_qkv[:, :qw]),
                dot_nt(gk, b_qkv[:, qw : qw + kw]),
                dot_nt(gv, b_qkv[:, qw + kw :]),
            ],
            axis=1,
        ).astype(BF16)
        * mask_three
    )
    grad_in_qkv = dot_tn(normed, grad_rank_qkv)
    grad_normed = dot_nt(grad_pre, project) + dot_nt(grad_rank_qkv, a_qkv)
    input_grad = (grad_hidden + norm_back(grad_normed, residual, inverse_one, attention_gain)).astype(BF16)

    rows = layer_input.shape[1] // shards

    def reduced(parts):
        flat = jnp.concatenate([p.astype(BF16).reshape(-1) for p in parts]).reshape(-1, 128)
        total = lax.psum(flat, ("rep", "shard")).reshape(-1)
        outs, at = [], 0
        for p in parts:
            outs.append(total[at : at + p.size].reshape(p.shape).astype(F32))
            at += p.size
        return outs

    t_in_out, t_out_out, t_in_router, t_out_router = reduced(
        [grad_in_out, grad_out_out, grad_in_router, grad_out_router]
    )
    grad_in_qkv, t_out_out = lax.optimization_barrier((grad_in_qkv, t_out_out))
    t_in_qkv, t_out_qkv = reduced([grad_in_qkv, grad_out_qkv])

    def part(x, axis):
        size = x.shape[axis] // shards
        return lax.dynamic_slice_in_dim(x, me * size, size, axis)

    total = lora_total.astype(F32)
    hidden = EXPERT_HIDDEN
    down_t = jnp.concatenate([total[:, 4 * rank :, :hidden], total[:, 4 * rank :, hidden:]], axis=1)
    return (
        block_out,
        input_grad,
        part(t_in_qkv, 0),
        part(t_out_qkv, 1),
        part(t_in_out, 0),
        part(t_out_out, 1),
        part(t_in_router, 0),
        part(t_out_router, 1),
        total[:, : 2 * rank].swapaxes(1, 2),
        total[:, 2 * rank : 3 * rank],
        down_t.swapaxes(1, 2),
        total[:, 3 * rank : 4 * rank],
    )


def solution(mesh):
    return jax.shard_map(
        local,
        mesh=mesh,
        in_specs=(
            P(("rep", "shard"), None),
            P(("rep", "shard"), None),
            P(("rep", "shard"), None),
            P("rep", None),
            P(),
            P(),
            P(None, "shard"),
            P("shard", None),
            P("shard", None),
            P("shard", None),
            P(None, "shard"),
            P("shard", None),
            P(None, "shard"),
            P("shard", None),
            P(None, "shard"),
            P("shard", None, None),
            P("shard", None, None),
            P("shard", None, None),
            P("shard", None, None),
            P("shard", None, None),
            P("shard", None, None),
        ),
        out_specs=(
            P(("rep", "shard"), None),
            P(("rep", "shard"), None),
            P("shard", None),
            P(None, "shard"),
            P("shard", None),
            P(None, "shard"),
            P("shard", None),
            P(None, "shard"),
            P("shard", None, None),
            P("shard", None, None),
            P("shard", None, None),
            P("shard", None, None),
        ),
        check_vma=False,
    )
```
